32 devices in a mesh: grp: 2 (over x), res: 16 (over z, y, core).
Axes of the slice: x: 2, y: 2, z: 4, core: 2. Of those that a mesh axis runs over, the one named last changes fastest.
Arguments:
- alignment_activations: bfloat16 [128, 128, 256], P('grp', 'res'), parts along dimension 0, may hold values from -6 to 6
- projection_weight: bfloat16 [256, 64], replicated, may hold values from -0.375 to 0.375
- output_weight: bfloat16 [1024, 128], replicated, may hold values from -0.1875 to 0.1875
- output_bias: float32 [128], replicated, may hold values from -3 to 3
- pair_update_gradient: bfloat16 [256, 128, 128], P(('grp', 'res')), parts along dimension 0, may hold values from -6 to 6
- sequence_mask: int32 [128], P('grp'), parts along dimension 0, may hold values 0 or 1
- residue_mask: int32 [256], P('grp'), parts along dimension 0, may hold values 0 or 1
Outputs:
- pair_increment: bfloat16 [256, 128, 128], P(('grp', 'res')), parts along dimension 0
- alignment_gradient: bfloat16 [128, 128, 256], P('grp', 'res'), parts along dimension 0
The draws below stay inside these ranges and needn't reach their ends.
There are 2 independent parts, one for each index of `grp`. The reference program is written for one: setup_inputs(seed, part) draws one part's arguments, and reference() takes and returns one part's arrays. A program takes and returns all parts, laid end to end along the dimension named above; an argument that names none is the same for every part. Nothing has to cross between parts.
All inputs are finite; a program needn't handle non-finite values.
Results may differ from the reference program's by a relative error of at most 0.007.
Values may be sent and summed in bfloat16 or wider, within the bound.
No kernel may reach another device: no remote copies, remote signals or barrier semaphores. Data moves between devices by JAX's collectives and lax.ppermute only.
A program may use at most 64 MiB of HBM per device.

```python
import jax
import jax.numpy as jnp
from jax import lax

ALIGNED_CHANNELS = 256
PROJECTED_WIDTH = 32
PAIR_WIDTH = 128
ALIGNED_SEQS = 64
RESIDUES_LOCAL = 8
RESIDUE_TOTAL = 128


def plant(drawn, own_key, low, largest):
    spot = [jax.random.randint(jax.random.fold_in(own_key, axis), (), 0, length) for axis, length in enumerate(drawn.shape)]
    widest = drawn.shape.index(max(drawn.shape))
    next_to = spot[:widest] + [(spot[widest] + 1) % drawn.shape[widest]] + spot[widest + 1:]
    return drawn.at[tuple(spot)].set(low).at[tuple(next_to)].set(largest)


def raised(drawn, stream_key, source, target, blocks, factor):
    def block_of(position):
        return (jnp.arange(drawn.shape[position]) // (drawn.shape[position] // blocks)).reshape((-1,) + (1,) * (drawn.ndim - 1 - position))

    first = jax.random.permutation(stream_key, blocks)[block_of(target)]
    second = (block_of(target) + blocks // 2) % blocks
    return jnp.where((block_of(source) == first) | (block_of(source) == second), factor * drawn, drawn)


def block_scale(own_key, shape, shards, smallest, high):
    level, own = 1.0, jax.random.fold_in(own_key, 6)
    for dim, parts in shards:
        steps = jnp.exp(jax.random.uniform(jax.random.fold_in(own, dim), (parts,), jnp.float32, smallest / len(shards), high / len(shards)))
        level = level * jnp.repeat(steps, shape[dim] // parts).reshape([-1 if axis == dim else 1 for axis in range(len(shape))])
    return level


def bell_draw(own_key, dims, deviation, reach, split=(), kind=jnp.bfloat16):
    factor_of = block_scale(own_key, dims, split, -0.22, 0.18) if split else 1.0
    drawn = jax.random.normal(own_key, dims, jnp.float32) * deviation * factor_of
    return jnp.minimum(jnp.maximum(drawn, -reach), reach).astype(kind)


def noise_with(stream_key, extent, scale, most, split, heavy, dtype=jnp.bfloat16):
    result = scale * jax.random.normal(stream_key, extent, jnp.float32)
    if split:
        result = result * block_scale(stream_key, extent, split, -0.22, 0.18)
    return jnp.clip(raised(result, jax.random.fold_in(stream_key, 3), *heavy), -most, most).astype(dtype)


def setup_inputs(seed: int = 0, part: int = 0) -> dict:
    arg_keys = jax.random.split(jax.random.key(seed), 8)
    part_splits = jax.random.split(jax.random.fold_in(arg_keys[7], part), 8)
    alignment_activations = bell_draw(part_splits[0], (ALIGNED_SEQS, RESIDUE_TOTAL, ALIGNED_CHANNELS), 1.0, 6.0, ((1, 16),))
    projection_weight = bell_draw(arg_keys[1], (ALIGNED_CHANNELS, 2 * PROJECTED_WIDTH), ALIGNED_CHANNELS ** -0.5, 0.375)
    output_weight = bell_draw(arg_keys[2], (PROJECTED_WIDTH * PROJECTED_WIDTH, PAIR_WIDTH), (PROJECTED_WIDTH * PROJECTED_WIDTH) ** -0.5, 0.1875)
    output_bias = bell_draw(arg_keys[3], (PAIR_WIDTH,), 0.5, 3.0, (), jnp.float32)
    pair_update_gradient = noise_with(part_splits[4], (RESIDUE_TOTAL, RESIDUE_TOTAL, PAIR_WIDTH), 1.0, 6.0, ((0, 16),), (0, 1, 16, 2.0))
    sequence_mask = plant((jax.random.randint(part_splits[5], (ALIGNED_SEQS,), 0, 4) < 3).astype(jnp.int32), jax.random.fold_in(part_splits[5], 1), 0, 1)
    residue_mask = plant((jax.random.randint(part_splits[6], (RESIDUE_TOTAL,), 0, 8) < 7).astype(jnp.int32), jax.random.fold_in(part_splits[6], 1), 0, 1)
    return dict(alignment_activations=alignment_activations, projection_weight=projection_weight, output_weight=output_weight, output_bias=output_bias, pair_update_gradient=pair_update_gradient, sequence_mask=sequence_mask, residue_mask=residue_mask)


eps_norm = 1e-05

def layer_norm_forward(values):
    mean_val = lax.optimization_barrier(jnp.mean(values, axis=-1, keepdims=True))
    centered = values - mean_val
    inverse_deviation = lax.rsqrt(lax.optimization_barrier(jnp.mean(centered * centered, axis=-1, keepdims=True)) + eps_norm)
    return (centered * inverse_deviation, inverse_deviation)

def layer_norm_backward(grad_out, scaled_product, inverse_deviation):
    mean_grad = lax.optimization_barrier(jnp.mean(grad_out, axis=-1, keepdims=True))
    mean_cross = lax.optimization_barrier(jnp.mean(grad_out * scaled_product, axis=-1, keepdims=True))
    return inverse_deviation * (grad_out - mean_grad - scaled_product * mean_cross)

def reference(alignment_activations, projection_weight, output_weight, output_bias, pair_update_gradient, sequence_mask, residue_mask):
    scaled_product, inverse_deviation = layer_norm_forward(alignment_activations.astype(jnp.float32))
    normalized_input = scaled_product.astype(jnp.bfloat16)
    residue_float_mask = residue_mask.astype(jnp.float32)
    alignment_mask = sequence_mask.astype(jnp.float32)[:, None] * residue_float_mask[None, :]
    projected_rows = jnp.dot(normalized_input.reshape(-1, ALIGNED_CHANNELS), projection_weight, preferred_element_type=jnp.float32)
    projected_rows = projected_rows.reshape(ALIGNED_SEQS, RESIDUE_TOTAL, 2 * PROJECTED_WIDTH) * alignment_mask[:, :, None]
    projected_rows = projected_rows.astype(jnp.bfloat16)
    left_projected = projected_rows[:, :, :PROJECTED_WIDTH]
    right_proj = projected_rows[:, :, PROJECTED_WIDTH:]
    live_rows = jnp.sum(sequence_mask.astype(jnp.float32))
    right_wide = right_proj.astype(jnp.float32)
    block_count = RESIDUE_TOTAL // RESIDUES_LOCAL
    left_pieces = left_projected.reshape(ALIGNED_SEQS, block_count, RESIDUES_LOCAL, PROJECTED_WIDTH).transpose(1, 0, 2, 3)
    cot_blocks = pair_update_gradient.reshape(block_count, RESIDUES_LOCAL, RESIDUE_TOTAL, PAIR_WIDTH)
    mask_blocks = residue_float_mask.reshape(block_count, RESIDUES_LOCAL)

    def step_block(right_gradient, inputs):
        left_blk, cot_blk, mask_blk = inputs
        pair_count = jnp.maximum(live_rows * mask_blk[:, None] * residue_float_mask[None, :], 1.0)
        left_wide = left_blk.astype(jnp.float32)
        outer = jnp.einsum('sic,sjd->ijcd', left_wide, right_wide).astype(jnp.bfloat16)
        update = jnp.dot(outer.reshape(-1, PROJECTED_WIDTH * PROJECTED_WIDTH), output_weight, preferred_element_type=jnp.float32)
        update = update.reshape(RESIDUES_LOCAL, RESIDUE_TOTAL, PAIR_WIDTH) + output_bias[None, None, :]
        update = (update / pair_count[:, :, None]).astype(jnp.bfloat16)
        grad_outer = jnp.dot(cot_blk.reshape(-1, PAIR_WIDTH), output_weight.T, preferred_element_type=jnp.float32)
        grad_outer = grad_outer.reshape(RESIDUES_LOCAL, RESIDUE_TOTAL, PROJECTED_WIDTH, PROJECTED_WIDTH) / pair_count[:, :, None, None]
        grad_outer = lax.optimization_barrier(grad_outer.astype(jnp.bfloat16)).astype(jnp.float32)
        left_gradient = jnp.einsum('ijcd,sjd->sic', grad_outer, right_wide)
        right_gradient = right_gradient + jnp.einsum('ijcd,sic->sjd', grad_outer, left_wide)
        return (right_gradient, (update, left_gradient))
    initial_gradient = jnp.zeros((ALIGNED_SEQS, RESIDUE_TOTAL, PROJECTED_WIDTH), jnp.float32)
    right_gradient, (updates, left_gradients) = lax.scan(step_block, initial_gradient, (left_pieces, cot_blocks, mask_blocks))
    pair_increment = updates.reshape(RESIDUE_TOTAL, RESIDUE_TOTAL, PAIR_WIDTH)
    left_gradient = left_gradients.transpose(1, 0, 2, 3).reshape(ALIGNED_SEQS, RESIDUE_TOTAL, PROJECTED_WIDTH)
    projection_gradient = jnp.concatenate([left_gradient, right_gradient], axis=-1) * alignment_mask[:, :, None]
    projection_gradient = projection_gradient.astype(jnp.bfloat16)
    normalized_gradient = jnp.dot(projection_gradient.reshape(-1, 2 * PROJECTED_WIDTH), projection_weight.T, preferred_element_type=jnp.float32)
    normalized_gradient = normalized_gradient.reshape(ALIGNED_SEQS, RESIDUE_TOTAL, ALIGNED_CHANNELS)
    alignment_gradient = layer_norm_backward(normalized_gradient, scaled_product, inverse_deviation).astype(jnp.bfloat16)
    return (pair_increment, alignment_gradient)
```

```python
import functools

import jax
import jax.numpy as jnp
from jax import lax
from jax.experimental import pallas as pl
from jax.experimental.pallas import tpu as pltpu
from jax.sharding import PartitionSpec as P

eps_norm = 1e-05
F32, BF16 = jnp.float32, jnp.bfloat16
LANES = 128
NT = (((1,), (1,)), ((), ()))
TN = (((0,), (0,)), ((), ()))


def dot(a, b, dims=(((1,), (0,)), ((), ()))):
    return lax.dot_general(a, b, dims, preferred_element_type=F32)


def exchange_masks(size):
    return [1 << k for k in range(size.bit_length() - 1)]


def block_masks(size):
    masks = exchange_masks(size)
    order = []
    for m in range(size):
        mask = 0
        for k, b in enumerate(masks):
            if (m >> (len(masks) - 1 - k)) & 1:
                mask ^= b
        order.append(mask)
    return order


def pack_mask(seq_ref, residue_of, count):
    seqs = seq_ref.shape[1]
    per = LANES // seqs
    seq = jnp.concatenate([seq_ref[...].astype(F32)] * per, axis=1)
    lane = lax.broadcasted_iota(jnp.int32, (1, LANES), 1)
    tiles = []
    for q in range(count // per):
        live = jnp.zeros((1, LANES), F32)
        for k in range(per):
            here = (lane >= k * seqs) & (lane < (k + 1) * seqs)
            live = jnp.where(here, residue_of(q * per + k), live)
        tiles.append(seq * live)
    return tiles


def project_kernel(x_ref, w_ref, seq_ref, res_ref, rloc_ref, left_ref, scaled_ref, inv_ref, rows, invs, zs):
    seqs, local, width = x_ref.shape
    chans = w_ref.shape[0] // 2
    half = chans // 2
    me = lax.axis_index("res")
    x = x_ref[...].astype(F32).reshape(seqs * local, width)
    cen = x - jnp.mean(x, axis=-1, keepdims=True)
    inv = lax.rsqrt(jnp.mean(cen * cen, axis=-1, keepdims=True) + eps_norm)
    scaled = cen * inv
    for h in range(width // LANES):
        rows[h] = scaled[:, h * LANES : (h + 1) * LANES]
    invs[...] = jnp.broadcast_to(inv, invs.shape)
    for j in range(local):
        for h in range(width // LANES):
            scaled_ref[j * seqs : (j + 1) * seqs, h * LANES : (h + 1) * LANES] = rows[
                h, pl.ds(j, seqs, stride=local), :
            ]
        inv_ref[j * seqs : (j + 1) * seqs, :] = invs[pl.ds(j, seqs, stride=local), :]
    pt = dot(w_ref[...], scaled_ref[...].astype(BF16), NT)
    mask = pack_mask(seq_ref, lambda j: res_ref[me * local + j].astype(F32), local)
    pt = pt * jnp.concatenate(mask, axis=1)
    left_ref[...] = pt[:chans].T.astype(BF16)
    lane = lax.broadcasted_iota(jnp.int32, (half, LANES), 1)
    for q in range(local // 2):
        lo = pt[chans : chans + half, q * LANES : (q + 1) * LANES]
        hi = pt[chans + half :, q * LANES : (q + 1) * LANES]
        zs[2 * q * half : (2 * q + 1) * half, :] = jnp.where(lane < seqs, lo, pltpu.roll(hi, seqs, 1))
        zs[(2 * q + 1) * half : (2 * q + 2) * half, :] = jnp.where(lane < seqs, pltpu.roll(lo, seqs, 1), hi)
    for dd in range(half):
        rloc_ref[:, dd * LANES : (dd + 1) * LANES] = zs[pl.ds(dd, local, stride=half), :].astype(BF16)


def pull_kernel(order, left_ref, wo_ref, g_ref, lp_ref, keep_ref, send_ref, grel_ref, wd_ref, w32, g32):
    local, total, pair = g_ref.shape
    chans = left_ref.shape[1]
    seqs = left_ref.shape[0] // local
    half = chans // 2
    me = lax.axis_index("res")
    w32[...] = wo_ref[...].astype(F32)
    for d in range(chans):
        wd_ref[d * chans : (d + 1) * chans, :] = w32[pl.ds(d, chans, stride=chans), :].astype(BF16)
    g32[...] = g_ref[...].astype(F32)
    for m in range(0, len(order), 2):
        one = pl.multiple_of((me ^ order[m]) * local, local)
        two = pl.multiple_of((me ^ order[m + 1]) * local, local)
        for i in range(local):
            block = jnp.concatenate([g32[i, pl.ds(one, local), :], g32[i, pl.ds(two, local), :]], axis=0)
            grel_ref[m * local : (m + 2) * local, i * pair : (i + 1) * pair] = block.astype(BF16)
    left = left_ref[...]
    mid = total // 2
    for dd in range(0, half, 2):
        for k in (dd, dd + 1):
            w = jnp.concatenate(
                [wd_ref[k * chans : (k + 1) * chans, :], wd_ref[(k + half) * chans : (k + half + 1) * chans, :]],
                axis=1,
            )
            x = dot(left, w).astype(BF16)
            for i in range(local):
                for h in range(2):
                    lp_ref[k * LANES + h * seqs : k * LANES + (h + 1) * seqs, i * pair : (i + 1) * pair] = x[
                        i * seqs : (i + 1) * seqs, h * pair : (h + 1) * pair
                    ]
        cols = slice(dd * LANES, (dd + 2) * LANES)
        part = dot(grel_ref[...], lp_ref[cols, :], NT)
        keep_ref[:, cols] = part[:mid]
        send_ref[:, cols] = part[mid:].astype(BF16)


def relative_row(row, order, me, local, col, rel):
    total = row.shape[1]
    col[...] = jnp.broadcast_to(row, (LANES, total)).T
    for m, mask in enumerate(order):
        rel[m * local : (m + 1) * local, :] = col[pl.ds(pl.multiple_of((me ^ mask) * local, local), local), :]
    return rel[...].T[:1, :]


def outer_grad_kernel(order, wd_ref, grel_ref, seq_ref, res_ref, ress_ref, got_ref, col, rel):
    total = grel_ref.shape[0]
    pair = wd_ref.shape[1]
    local = grel_ref.shape[1] // pair
    chans = got_ref.shape[0] // (2 * local)
    half = chans // 2
    me = lax.axis_index("res")
    live = jnp.sum(seq_ref[...].astype(F32))
    live_row = relative_row(res_ref[...].astype(F32), order, me, local, col, rel) * live
    for i in range(local):
        count = jnp.maximum(live_row * ress_ref[me * local + i].astype(F32), 1.0)
        t = dot(wd_ref[...], grel_ref[:, i * pair : (i + 1) * pair], NT) * (1.0 / count)
        t = t.astype(BF16)
        for d in range(chans):
            h, dd = divmod(d, half)
            got_ref[(h * local + i) * chans : (h * local + i + 1) * chans, dd * total : (dd + 1) * total] = t[
                d * chans : (d + 1) * chans, :
            ]


def pair_kernel(order, r_ref, lp_ref, got_ref, bias_ref, seq_ref, res_ref, ress_ref, pair_ref, gl_ref, ubuf):
    local, total, pair = pair_ref.shape
    half = r_ref.shape[1] // LANES
    me = lax.axis_index("res")
    live = jnp.sum(seq_ref[...].astype(F32))
    acc = None
    for dd in range(0, half, 2):
        rows = jnp.concatenate(
            [r_ref[:, dd * LANES : (dd + 1) * LANES], r_ref[:, (dd + 1) * LANES : (dd + 2) * LANES]], axis=0
        )
        t = dot(got_ref[:, dd * total : (dd + 2) * total], rows)
        acc = t if acc is None else acc + t
    gl_ref[...] = acc
    live_col = jnp.broadcast_to(res_ref[...].astype(F32) * live, (LANES, total)).T
    bias = bias_ref[...]
    for i in range(0, local, 2):
        u = dot(r_ref[...], lp_ref[:, i * pair : (i + 2) * pair])
        for m, mask in enumerate(order):
            ubuf[pl.ds(pl.multiple_of((me ^ mask) * local, local), local), :] = u[m * local : (m + 1) * local, :]
        for k in range(2):
            count = jnp.maximum(live_col * ress_ref[me * local + i + k].astype(F32), 1.0)
            pair_ref[i + k] = ((ubuf[:, k * pair : (k + 1) * pair] + bias) * (1.0 / count)).astype(BF16)


def final_kernel(gl_ref, gr_ref, scaled_ref, inv_ref, w_ref, seq_ref, res_ref, out_ref, zs, proj, rows):
    seqs, local, width = out_ref.shape
    chans = w_ref.shape[0] // 2
    half = chans // 2
    me = lax.axis_index("res")
    live = jnp.sum(seq_ref[...].astype(F32))
    for dd in range(half):
        zs[pl.ds(dd, local, stride=half), :] = gr_ref[:, dd * LANES : (dd + 1) * LANES]

    def scale_of(j):
        keep = res_ref[me * local + j].astype(F32)
        return keep / jnp.maximum(live * keep, 1.0)

    mask = pack_mask(seq_ref, lambda j: res_ref[me * local + j].astype(F32), local)
    scale = pack_mask(seq_ref, scale_of, local)
    lane_c = lax.broadcasted_iota(jnp.int32, (chans, LANES), 1) < seqs
    lane_h = lax.broadcasted_iota(jnp.int32, (half, LANES), 1) < seqs
    for q in range(local // 2):
        cols = slice(q * LANES, (q + 1) * LANES)
        a, b = 2 * q, 2 * q + 1
        lo_a = gl_ref[a * chans : (a + 1) * chans, :]
        hi_a = gl_ref[(local + a) * chans : (local + a + 1) * chans, :]
        lo_b = gl_ref[b * chans : (b + 1) * chans, :]
        hi_b = gl_ref[(local + b) * chans : (local + b + 1) * chans, :]
        left = jnp.where(lane_c, lo_a + pltpu.roll(hi_a, seqs, 1), pltpu.roll(lo_b, seqs, 1) + hi_b)
        proj[:chans, cols] = (left * mask[q]).astype(BF16)
        za = zs[a * half : (a + 1) * half, :]
        zb = zs[b * half : (b + 1) * half, :]
        low = jnp.where(lane_h, za, pltpu.roll(zb, seqs, 1))
        high = jnp.where(lane_h, pltpu.roll(za, seqs, 1), zb)
        proj[chans : chans + half, cols] = (low * scale[q]).astype(BF16)
        proj[chans + half :, cols] = (high * scale[q]).astype(BF16)
    grad = dot(proj[...], w_ref[...], TN)
    scaled = scaled_ref[...]
    inv = inv_ref[:, :1]
    mean_grad = jnp.mean(grad, axis=-1, keepdims=True)
    mean_cross = jnp.mean(grad * scaled, axis=-1, keepdims=True)
    res = inv * (grad - mean_grad - scaled * mean_cross)
    for j in range(local):
        for h in range(width // LANES):
            rows[h, pl.ds(j, seqs, stride=local), :] = res[
                j * seqs : (j + 1) * seqs, h * LANES : (h + 1) * LANES
            ]
    for h in range(width // LANES):
        out_ref[:, :, h * LANES : (h + 1) * LANES] = rows[h].reshape(seqs, local, LANES).astype(BF16)


def shape(dims, dtype):
    return jax.ShapeDtypeStruct(dims, dtype)


VM = pl.BlockSpec(memory_space=pltpu.VMEM)
SM = pl.BlockSpec(memory_space=pltpu.SMEM)


def body(size, acts, proj_w, out_w, out_b, cot, seq_mask, res_mask):
    seqs, local, width = acts.shape
    chans = proj_w.shape[1] // 2
    pair = out_w.shape[1]
    total = cot.shape[1]
    flat = chans * seqs
    half = chans // 2
    order = block_masks(size)
    masks = exchange_masks(size)
    proj_t = proj_w.T
    seq_row = seq_mask.reshape(1, seqs)
    res_row = res_mask.reshape(1, total)

    r, left, scaled, inv = pl.pallas_call(
        project_kernel,
        out_shape=(
            shape((local, flat), BF16),
            shape((local * seqs, chans), BF16),
            shape((local * seqs, width), F32),
            shape((local * seqs, LANES), F32),
        ),
        in_specs=[VM, VM, VM, SM],
        out_specs=(VM, VM, VM, VM),
        scratch_shapes=[
            pltpu.VMEM((width // LANES, seqs * local, LANES), F32),
            pltpu.VMEM((seqs * local, LANES), F32),
            pltpu.VMEM((local * half, LANES), F32),
        ],
        name="project",
    )(acts, proj_t, seq_row, res_mask)

    lp, keep, send, grel, wd = pl.pallas_call(
        functools.partial(pull_kernel, order),
        out_shape=(
            shape((flat, local * pair), BF16),
            shape((total // 2, flat), F32),
            shape((total // 2, flat), BF16),
            shape((total, local * pair), BF16),
            shape(out_w.shape, BF16),
        ),
        in_specs=[VM] * 3,
        out_specs=(VM,) * 5,
        scratch_shapes=[pltpu.VMEM(out_w.shape, F32), pltpu.VMEM(cot.shape, F32)],
        name="pull",
    )(left, out_w, cot)

    got = pl.pallas_call(
        functools.partial(outer_grad_kernel, order),
        out_shape=shape((2 * local * chans, half * total), BF16),
        in_specs=[VM, VM, VM, VM, SM],
        out_specs=VM,
        scratch_shapes=[pltpu.VMEM((total, LANES), F32), pltpu.VMEM((total, LANES), F32)],
        name="outer_grad",
    )(wd, grel, seq_row, res_row, res_mask)

    def swap(v, b):
        return lax.ppermute(v, "res", [(i, i ^ b) for i in range(size)])

    for b in reversed(masks):
        r = jnp.concatenate([r, swap(r, b)], axis=0)

    right = keep + swap(send, masks[0]).astype(F32)
    for b in masks[1:]:
        h = right.shape[0] // 2
        right = right[:h] + swap(right[h:].astype(BF16), b).astype(F32)

    pair_out, gl = pl.pallas_call(
        functools.partial(pair_kernel, order),
        out_shape=(shape((local, total, pair), BF16), shape((2 * local * chans, LANES), F32)),
        in_specs=[VM, VM, VM, VM, VM, VM, SM],
        out_specs=(VM, VM),
        scratch_shapes=[pltpu.VMEM((total, 2 * pair), F32)],
        name="pair",
    )(r, lp, got, out_b.reshape(1, pair), seq_row, res_row, res_mask)

    grad = pl.pallas_call(
        final_kernel,
        out_shape=shape(acts.shape, BF16),
        in_specs=[VM, VM, VM, VM, VM, VM, SM],
        out_specs=VM,
        scratch_shapes=[
            pltpu.VMEM((local * half, LANES), F32),
            pltpu.VMEM((2 * chans, local * seqs), BF16),
            pltpu.VMEM((width // LANES, seqs * local, LANES), F32),
        ],
        name="final",
    )(gl, right, scaled, inv, proj_t, seq_row, res_mask)
    return pair_out, grad


def solution(mesh):
    in_specs = (
        P("grp", "res", None),
        P(),
        P(),
        P(),
        P(("grp", "res"), None, None),
        P("grp"),
        P("grp"),
    )
    out_specs = (P(("grp", "res"), None, None), P("grp", "res", None))
    return jax.shard_map(
        functools.partial(body, mesh.shape["res"]),
        mesh=mesh,
        in_specs=in_specs,
        out_specs=out_specs,
        check_vma=False,
    )
```

```python
import functools

import jax
import jax.numpy as jnp
from jax import lax
from jax.experimental import pallas as pl
from jax.experimental.pallas import tpu as pltpu
from jax.sharding import PartitionSpec as P

eps_norm = 1e-05
F32, BF16 = jnp.float32, jnp.bfloat16
LANES = 128
NT = (((1,), (1,)), ((), ()))
TN = (((0,), (0,)), ((), ()))


def dot(a, b, dims=(((1,), (0,)), ((), ()))):
    return lax.dot_general(a, b, dims, preferred_element_type=F32)


def exchange_masks(size):
    return [1 << k for k in range(size.bit_length() - 1)]


def block_masks(size):
    masks = exchange_masks(size)
    order = []
    for m in range(size):
        mask = 0
        for k, b in enumerate(masks):
            if (m >> (len(masks) - 1 - k)) & 1:
                mask ^= b
        order.append(mask)
    return order


def pack_mask(seq_ref, residue_of, count):
    seqs = seq_ref.shape[1]
    per = LANES // seqs
    seq = jnp.concatenate([seq_ref[...].astype(F32)] * per, axis=1)
    lane = lax.broadcasted_iota(jnp.int32, (1, LANES), 1)
    tiles = []
    for q in range(count // per):
        live = jnp.zeros((1, LANES), F32)
        for k in range(per):
            here = (lane >= k * seqs) & (lane < (k + 1) * seqs)
            live = jnp.where(here, residue_of(q * per + k), live)
        tiles.append(seq * live)
    return tiles


def project_kernel(x_ref, w_ref, seq_ref, res_ref, rloc_ref, left_ref, scaled_ref, inv_ref, rows, invs, zs):
    seqs, local, width = x_ref.shape
    chans = w_ref.shape[0] // 2
    half = chans // 2
    me = lax.axis_index("res")
    x = x_ref[...].astype(F32).reshape(seqs * local, width)
    cen = x - jnp.mean(x, axis=-1, keepdims=True)
    inv = lax.rsqrt(jnp.mean(cen * cen, axis=-1, keepdims=True) + eps_norm)
    scaled = cen * inv
    for h in range(width // LANES):
        rows[h] = scaled[:, h * LANES : (h + 1) * LANES]
    invs[...] = jnp.broadcast_to(inv, invs.shape)
    for j in range(local):
        for h in range(width // LANES):
            scaled_ref[j * seqs : (j + 1) * seqs, h * LANES : (h + 1) * LANES] = rows[
                h, pl.ds(j, seqs, stride=local), :
            ]
        inv_ref[j * seqs : (j + 1) * seqs, :] = invs[pl.ds(j, seqs, stride=local), :]
    pt = dot(w_ref[...], scaled_ref[...].astype(BF16), NT)
    mask = pack_mask(seq_ref, lambda j: res_ref[me * local + j].astype(F32), local)
    pt = pt * jnp.concatenate(mask, axis=1)
    left_ref[...] = pt[:chans].T.astype(BF16)
    lane = lax.broadcasted_iota(jnp.int32, (half, LANES), 1)
    for q in range(local // 2):
        lo = pt[chans : chans + half, q * LANES : (q + 1) * LANES]
        hi = pt[chans + half :, q * LANES : (q + 1) * LANES]
        zs[2 * q * half : (2 * q + 1) * half, :] = jnp.where(lane < seqs, lo, pltpu.roll(hi, seqs, 1))
        zs[(2 * q + 1) * half : (2 * q + 2) * half, :] = jnp.where(lane < seqs, pltpu.roll(lo, seqs, 1), hi)
    for dd in range(half):
        rloc_ref[:, dd * LANES : (dd + 1) * LANES] = zs[pl.ds(dd, local, stride=half), :].astype(BF16)


def pull_kernel(order, left_ref, wo_ref, g_ref, lp_ref, keep_ref, send_ref, grel_ref, wd_ref, w32, g32):
    local, total, pair = g_ref.shape
    chans = left_ref.shape[1]
    seqs = left_ref.shape[0] // local
    half = chans // 2
    me = lax.axis_index("res")
    w32[...] = wo_ref[...].astype(F32)
    for d in range(chans):
        wd_ref[d * chans : (d + 1) * chans, :] = w32[pl.ds(d, chans, stride=chans), :].astype(BF16)
    g32[...] = g_ref[...].astype(F32)
    for m in range(0, len(order), 2):
        one = pl.multiple_of((me ^ order[m]) * local, local)
        two = pl.multiple_of((me ^ order[m + 1]) * local, local)
        for i in range(local):
            block = jnp.concatenate([g32[i, pl.ds(one, local), :], g32[i, pl.ds(two, local), :]], axis=0)
            grel_ref[m * local : (m + 2) * local, i * pair : (i + 1) * pair] = block.astype(BF16)
    left = left_ref[...]
    mid = total // 2
    for dd in range(0, half, 2):
        for k in (dd, dd + 1):
            w = jnp.concatenate(
                [wd_ref[k * chans : (k + 1) * chans, :], wd_ref[(k + half) * chans : (k + half + 1) * chans, :]],
                axis=1,
            )
            x = dot(left, w).astype(BF16)
            for i in range(local):
                for h in range(2):
                    lp_ref[k * LANES + h * seqs : k * LANES + (h + 1) * seqs, i * pair : (i + 1) * pair] = x[
                        i * seqs : (i + 1) * seqs, h * pair : (h + 1) * pair
                    ]
        cols = slice(dd * LANES, (dd + 2) * LANES)
        part = dot(grel_ref[...], lp_ref[cols, :], NT)
        keep_ref[:, cols] = part[:mid]
        send_ref[:, cols] = part[mid:].astype(BF16)


def relative_row(row, order, me, local, col, rel):
    total = row.shape[1]
    col[...] = jnp.broadcast_to(row, (LANES, total)).T
    for m, mask in enumerate(order):
        rel[m * local : (m + 1) * local, :] = col[pl.ds(pl.multiple_of((me ^ mask) * local, local), local), :]
    return rel[...].T[:1, :]


def outer_grad_kernel(order, wd_ref, grel_ref, seq_ref, res_ref, ress_ref, got_ref, col, rel):
    total = grel_ref.shape[0]
    pair = wd_ref.shape[1]
    local = grel_ref.shape[1] // pair
    chans = got_ref.shape[0] // (2 * local)
    half = chans // 2
    me = lax.axis_index("res")
    live = jnp.sum(seq_ref[...].astype(F32))
    live_row = relative_row(res_ref[...].astype(F32), order, me, local, col, rel) * live
    for i in range(local):
        count = jnp.maximum(live_row * ress_ref[me * local + i].astype(F32), 1.0)
        t = dot(wd_ref[...], grel_ref[:, i * pair : (i + 1) * pair], NT) * (1.0 / count)
        t = t.astype(BF16)
        for d in range(chans):
            h, dd = divmod(d, half)
            got_ref[(h * local + i) * chans : (h * local + i + 1) * chans, dd * total : (dd + 1) * total] = t[
                d * chans : (d + 1) * chans, :
            ]


def pair_kernel(order, r_ref, lp_ref, got_ref, bias_ref, seq_ref, res_ref, ress_ref, pair_ref, gl_ref, ubuf):
    local, total, pair = pair_ref.shape
    half = r_ref.shape[1] // LANES
    me = lax.axis_index("res")
    live = jnp.sum(seq_ref[...].astype(F32))
    acc = None
    for dd in range(0, half, 2):
        rows = jnp.concatenate(
            [r_ref[:, dd * LANES : (dd + 1) * LANES], r_ref[:, (dd + 1) * LANES : (dd + 2) * LANES]], axis=0
        )
        t = dot(got_ref[:, dd * total : (dd + 2) * total], rows)
        acc = t if acc is None else acc + t
    gl_ref[...] = acc
    live_col = jnp.broadcast_to(res_ref[...].astype(F32) * live, (LANES, total)).T
    bias = bias_ref[...]
    for i in range(0, local, 2):
        u = dot(r_ref[...], lp_ref[:, i * pair : (i + 2) * pair])
        for m, mask in enumerate(order):
            ubuf[pl.ds(pl.multiple_of((me ^ mask) * local, local), local), :] = u[m * local : (m + 1) * local, :]
        for k in range(2):
            count = jnp.maximum(live_col * ress_ref[me * local + i + k].astype(F32), 1.0)
            pair_ref[i + k] = ((ubuf[:, k * pair : (k + 1) * pair] + bias) * (1.0 / count)).astype(BF16)


def final_kernel(gl_ref, gr_ref, scaled_ref, inv_ref, w_ref, seq_ref, res_ref, out_ref, zs, proj, rows):
    seqs, local, width = out_ref.shape
    chans = w_ref.shape[0] // 2
    half = chans // 2
    me = lax.axis_index("res")
    live = jnp.sum(seq_ref[...].astype(F32))
    for dd in range(half):
        zs[pl.ds(dd, local, stride=half), :] = gr_ref[:, dd * LANES : (dd + 1) * LANES]

    def scale_of(j):
        keep = res_ref[me * local + j].astype(F32)
        return keep / jnp.maximum(live * keep, 1.0)

    mask = pack_mask(seq_ref, lambda j: res_ref[me * local + j].astype(F32), local)
    scale = pack_mask(seq_ref, scale_of, local)
    lane_c = lax.broadcasted_iota(jnp.int32, (chans, LANES), 1) < seqs
    lane_h = lax.broadcasted_iota(jnp.int32, (half, LANES), 1) < seqs
    for q in range(local // 2):
        cols = slice(q * LANES, (q + 1) * LANES)
        a, b = 2 * q, 2 * q + 1
        lo_a = gl_ref[a * chans : (a + 1) * chans, :]
        hi_a = gl_ref[(local + a) * chans : (local + a + 1) * chans, :]
        lo_b = gl_ref[b * chans : (b + 1) * chans, :]
        hi_b = gl_ref[(local + b) * chans : (local + b + 1) * chans, :]
        left = jnp.where(lane_c, lo_a + pltpu.roll(hi_a, seqs, 1), pltpu.roll(lo_b, seqs, 1) + hi_b)
        proj[:chans, cols] = (left * mask[q]).astype(BF16)
        za = zs[a * half : (a + 1) * half, :]
        zb = zs[b * half : (b + 1) * half, :]
        low = jnp.where(lane_h, za, pltpu.roll(zb, seqs, 1))
        high = jnp.where(lane_h, pltpu.roll(za, seqs, 1), zb)
        proj[chans : chans + half, cols] = (low * scale[q]).astype(BF16)
        proj[chans + half :, cols] = (high * scale[q]).astype(BF16)
    grad = dot(proj[...], w_ref[...], TN)
    scaled = scaled_ref[...]
    inv = inv_ref[:, :1]
    mean_grad = jnp.mean(grad, axis=-1, keepdims=True)
    mean_cross = jnp.mean(grad * scaled, axis=-1, keepdims=True)
    res = inv * (grad - mean_grad - scaled * mean_cross)
    for j in range(local):
        for h in range(width // LANES):
            rows[h, pl.ds(j, seqs, stride=local), :] = res[
                j * seqs : (j + 1) * seqs, h * LANES : (h + 1) * LANES
            ]
    for h in range(width // LANES):
        out_ref[:, :, h * LANES : (h + 1) * LANES] = rows[h].reshape(seqs, local, LANES).astype(BF16)


def shape(dims, dtype):
    return jax.ShapeDtypeStruct(dims, dtype)


PARAMS = pltpu.CompilerParams(vmem_limit_bytes=16 * 1024 * 1024)
VM = pl.BlockSpec(memory_space=pltpu.VMEM)
SM = pl.BlockSpec(memory_space=pltpu.SMEM)


def body(size, acts, proj_w, out_w, out_b, cot, seq_mask, res_mask):
    seqs, local, width = acts.shape
    chans = proj_w.shape[1] // 2
    pair = out_w.shape[1]
    total = cot.shape[1]
    flat = chans * seqs
    half = chans // 2
    order = block_masks(size)
    masks = exchange_masks(size)
    proj_t = proj_w.T
    seq_row = seq_mask.reshape(1, seqs)
    res_row = res_mask.reshape(1, total)

    r, left, scaled, inv = pl.pallas_call(
        project_kernel,
        out_shape=(
            shape((local, flat), BF16),
            shape((local * seqs, chans), BF16),
            shape((local * seqs, width), F32),
            shape((local * seqs, LANES), F32),
        ),
        in_specs=[VM, VM, VM, SM],
        out_specs=(VM, VM, VM, VM),
        scratch_shapes=[
            pltpu.VMEM((width // LANES, seqs * local, LANES), F32),
            pltpu.VMEM((seqs * local, LANES), F32),
            pltpu.VMEM((local * half, LANES), F32),
        ],
        compiler_params=PARAMS,
        name="project",
    )(acts, proj_t, seq_row, res_mask)

    lp, keep, send, grel, wd = pl.pallas_call(
        functools.partial(pull_kernel, order),
        out_shape=(
            shape((flat, local * pair), BF16),
            shape((total // 2, flat), F32),
            shape((total // 2, flat), BF16),
            shape((total, local * pair), BF16),
            shape(out_w.shape, BF16),
        ),
        in_specs=[VM] * 3,
        out_specs=(VM,) * 5,
        scratch_shapes=[pltpu.VMEM(out_w.shape, F32), pltpu.VMEM(cot.shape, F32)],
        compiler_params=PARAMS,
        name="pull",
    )(left, out_w, cot)

    got = pl.pallas_call(
        functools.partial(outer_grad_kernel, order),
        out_shape=shape((2 * local * chans, half * total), BF16),
        in_specs=[VM, VM, VM, VM, SM],
        out_specs=VM,
        scratch_shapes=[pltpu.VMEM((total, LANES), F32), pltpu.VMEM((total, LANES), F32)],
        compiler_params=PARAMS,
        name="outer_grad",
    )(wd, grel, seq_row, res_row, res_mask)

    def swap(v, b):
        return lax.ppermute(v, "res", [(i, i ^ b) for i in range(size)])

    for b in reversed(masks):
        r = jnp.concatenate([r, swap(r, b)], axis=0)

    right = keep + swap(send, masks[0]).astype(F32)
    for b in masks[1:]:
        h = right.shape[0] // 2
        right = right[:h] + swap(right[h:].astype(BF16), b).astype(F32)

    pair_out, gl = pl.pallas_call(
        functools.partial(pair_kernel, order),
        out_shape=(shape((local, total, pair), BF16), shape((2 * local * chans, LANES), F32)),
        in_specs=[VM, VM, VM, VM, VM, VM, SM],
        out_specs=(VM, VM),
        scratch_shapes=[pltpu.VMEM((total, 2 * pair), F32)],
        compiler_params=PARAMS,
        name="pair",
    )(r, lp, got, out_b.reshape(1, pair), seq_row, res_row, res_mask)

    grad = pl.pallas_call(
        final_kernel,
        out_shape=shape(acts.shape, BF16),
        in_specs=[VM, VM, VM, VM, VM, VM, SM],
        out_specs=VM,
        scratch_shapes=[
            pltpu.VMEM((local * half, LANES), F32),
            pltpu.VMEM((2 * chans, local * seqs), BF16),
            pltpu.VMEM((width // LANES, seqs * local, LANES), F32),
        ],
        compiler_params=PARAMS,
        name="final",
    )(gl, right, scaled, inv, proj_t, seq_row, res_mask)
    return pair_out, grad


def solution(mesh):
    in_specs = (
        P("grp", "res", None),
        P(),
        P(),
        P(),
        P(("grp", "res"), None, None),
        P("grp"),
        P("grp"),
    )
    out_specs = (P(("grp", "res"), None, None), P("grp", "res", None))
    return jax.shard_map(
        functools.partial(body, mesh.shape["res"]),
        mesh=mesh,
        in_specs=in_specs,
        out_specs=out_specs,
        check_vma=False,
    )
```
